256 devices in a mesh: rep: 16 (over y_lo, z), tp: 16 (over x, y_hi, core).
Axes of the slice: x: 4, y: 4 (y_hi: 2, y_lo: 2; y = y_hi * 2 + y_lo), z: 8, core: 2. Of those that a mesh axis runs over, the one named last changes fastest.
Arguments:
- tokens: bfloat16 [16384, 8192], P('rep', 'tp'), may hold values from -6 to 6
- grad_out: bfloat16 [16384, 4096], P('rep', 'tp'), may hold values from -0.046875 to 0.046875
- lengths: int32 [16, 16], replicated, may hold values from 0 to 256, as said below
- master: float32 [8192, 2048], P('rep', 'tp'), may hold values from -3 to 3
- first: float32 [8192, 2048], P('rep', 'tp'), may hold values from -6 to 6
- second: float32 [8192, 2048], P('rep', 'tp'), may hold values from 0.25 to 4
Outputs:
- new_master: float32 [8192, 2048], P('rep', 'tp')
- new_first: float32 [8192, 2048], P('rep', 'tp')
- new_second: float32 [8192, 2048], P('rep', 'tp')
- healthy_weights: bfloat16 [8192, 2048], P(None, 'tp')
- slot_weights: bfloat16 [16, 8192, 4096], P('rep', None, 'tp')
The draws below stay inside these ranges and needn't reach their ends.
Inputs may be any that keep to these rules, and one draw needn't show every extreme that they name: `lengths`: each row is one replica's split of the 2048 columns over its devices in tp order: the entries are multiples of 64, sum to 2048, the nonzero ones come first and number at least half of the row; a row is either all 128 or has an entry equal to 256, and some row has an entry equal to 256.
All inputs are finite; a program needn't handle non-finite values.
Results may differ from the reference program's by a relative error of at most 0.0019.
Values may be sent and summed in bfloat16 or wider, within the bound.
No kernel may reach another device: no remote copies, remote signals or barrier semaphores. Data moves between devices by JAX's collectives and lax.ppermute only.
A program may use at most 128 MiB of HBM per device.

```python
import math
import jax
import jax.numpy as jnp
from jax import lax

D = 8192
COLS = 2048
TOK_DEV = 1024
STEP = 1000
TOKENS = 16384
MAXLEN = 256
N_REP = 16
N_TP = 16


def replica_split(key, counts):
    key_largest, key_order = jax.random.split(key)
    unit_width = COLS // (2 * N_TP)
    position = jnp.arange(N_TP, dtype=jnp.int32)
    largest = jax.random.randint(key_largest, (), 0, counts)
    scores = jax.random.permutation(key_order, N_TP)
    active = position < counts
    others = active & (position != largest)
    order_rank = jnp.sum(others[None, :] & (scores[None, :] < scores[:, None]), axis=1)
    spare_units = 2 * N_TP - 4 - (counts - 1)
    extra_units = jnp.clip(spare_units - 3 * order_rank, 0, 3)
    unit_counts = jnp.where(position == largest, 4, jnp.where(others, 1 + extra_units, 0))
    unit_counts = jnp.where(counts == N_TP, 2, unit_counts)
    return (unit_counts * unit_width).astype(jnp.int32)


def draw_lengths(key, part):
    keys = jax.random.split(jax.random.fold_in(key, 17), 3)
    counts = jax.random.randint(keys[0], (N_REP,), N_TP // 2, N_TP + 1)
    forced = jax.random.randint(keys[1], (), 0, N_REP)
    counts = jnp.where(jnp.arange(N_REP) == forced, N_TP // 2, counts)
    return jax.vmap(replica_split)(jax.random.split(keys[2], N_REP), counts)


def block_scale(key, dims, cuts, smallest, high):
    gain = 1.0
    for axis_at, shards_of in cuts:
        heights = jax.random.uniform(jax.random.fold_in(jax.random.fold_in(key, 6), axis_at), (shards_of,), jnp.float32, smallest / len(cuts), high / len(cuts))
        gain = gain * jnp.repeat(jnp.exp(heights), dims[axis_at] // shards_of).reshape((-1,) + (1,) * (len(dims) - 1 - axis_at))
    return gain


def gaussian(stream_key, dims, scale, reach, cuts=(), kind=jnp.bfloat16):
    level = block_scale(stream_key, dims, cuts, -0.22, 0.18) if cuts else 1.0
    array = jax.random.normal(stream_key, dims, jnp.float32) * scale * level
    return jnp.minimum(jnp.maximum(array, -reach), reach).astype(kind)


def setup_inputs(seed: int = 0) -> dict:
    arg_keys = jax.random.split(jax.random.key(seed), 7)
    tokens = gaussian(arg_keys[0], (TOKENS, D), 1.0, 6.0, ((0, 16), (1, 16)))
    grad_out = gaussian(arg_keys[1], (TOKENS, N_TP * MAXLEN), (TOK_DEV * N_REP) ** -0.5, 0.046875, ((0, 16), (1, 16)))
    lengths = draw_lengths(jax.random.fold_in(arg_keys[6], 71), 0)
    master = gaussian(arg_keys[3], (D, COLS), 0.5, 3.0, ((0, 16), (1, 16)), jnp.float32)
    first = gaussian(arg_keys[4], (D, COLS), 1.0, 6.0, ((0, 16), (1, 16)), jnp.float32)
    second = jnp.clip(jnp.exp(math.log(4.0) - 2.7725887 * jax.random.uniform(arg_keys[5], (D, COLS), jnp.float32) ** block_scale(arg_keys[5], (D, COLS), ((0, 16), (1, 16)), -0.2, 0.2)), 0.25, 4.0)
    return {"tokens": tokens, "grad_out": grad_out, "lengths": lengths, "master": master, "first": first, "second": second}


decay_first = 0.9
decay_second = 0.999
learning_rate = 0.02
weight_decay = 0.1
epsilon = 1e-08

def source(row_lengths, begins):
    columns = jnp.arange(COLS, dtype=jnp.int32)
    inside = (begins[None, :] <= columns[:, None]) & (columns[:, None] < (begins + row_lengths)[None, :])
    slot_index = jnp.arange(N_TP, dtype=jnp.int32)[None, :] * MAXLEN + columns[:, None] - begins[None, :]
    return lax.optimization_barrier(jnp.sum(jnp.where(inside, slot_index, 0), axis=1)).astype(jnp.int32)

def adam_update(master, first, second, gradient):
    scale_first = 1.0 - decay_first ** STEP
    scale_second = 1.0 - decay_second ** STEP
    new_first = decay_first * first + (1.0 - decay_first) * gradient
    new_second = decay_second * second + (1.0 - decay_second) * gradient * gradient
    direction = new_first / scale_first / (jnp.sqrt(new_second / scale_second) + epsilon)
    new_master = master - learning_rate * (direction + weight_decay * master)
    return (new_master, new_first, new_second)

def reference(tokens, grad_out, lengths, master, first, second):
    lengths = lengths.astype(jnp.int32)
    starts = (jnp.cumsum(lengths, axis=1) - lengths).astype(jnp.int32)
    token_blocks = tokens.reshape(N_REP, TOK_DEV, D)
    output_blocks = grad_out.reshape(N_REP, TOK_DEV, N_TP * MAXLEN)

    def accumulate(running, member):
        token_rows, grad_rows, row_lengths, begins = member
        dense_grad = jnp.take(grad_rows, source(row_lengths, begins), axis=1)
        return (running + jnp.dot(token_rows.T, dense_grad, preferred_element_type=jnp.float32), None)
    gradient = lax.scan(accumulate, jnp.zeros((D, COLS), jnp.float32), (token_blocks, output_blocks, lengths, starts))[0]
    new_master, new_first, new_second = adam_update(master, first, second, gradient)
    weights = new_master.astype(jnp.bfloat16)
    slot_pos = jnp.arange(N_TP * MAXLEN, dtype=jnp.int32)
    owner = (slot_pos // MAXLEN).astype(jnp.int32)
    within = (slot_pos % MAXLEN).astype(jnp.int32)

    def layout(member):
        row_lengths, begins = member
        column_src = (jnp.take(begins, owner) + within).astype(jnp.int32)
        valid = within < jnp.take(row_lengths, owner)
        picked = jnp.take(weights, jnp.clip(column_src, 0, COLS - 1), axis=1)
        return jnp.where(valid[None, :], picked, jnp.zeros_like(picked))
    slot_weights = lax.map(layout, (lengths, starts))
    return (new_master, new_first, new_second, weights, slot_weights)
```

```python
import jax
import jax.numpy as jnp
from jax import lax
from jax.experimental import pallas as pl
from jax.experimental.pallas import tpu as pltpu
from jax.sharding import Mesh
from jax.sharding import PartitionSpec as P

STEP = 1000
UNIT = 64
AXES = ("yl", "zh", "z0", "x", "yh", "co")
REP = ("yl", "zh", "z0")
TP = ("x", "yh", "co")
Z = ("zh", "z0")
GROUP = ("yl", "z0", "x", "yh", "co")
SWAP = [(0, 1), (1, 0)]

decay_first = 0.9
decay_second = 0.999
learning_rate = 0.02
weight_decay = 0.1
epsilon = 1e-08


def adam_update(master, first, second, gradient):
    scale_first = 1.0 - decay_first**STEP
    scale_second = 1.0 - decay_second**STEP
    new_first = decay_first * first + (1.0 - decay_first) * gradient
    new_second = decay_second * second + (1.0 - decay_second) * gradient * gradient
    direction = new_first / scale_first / (jnp.sqrt(new_second / scale_second) + epsilon)
    new_master = master - learning_rate * (direction + weight_decay * master)
    return (new_master, new_first, new_second)


def column_block(yl, z0, co, x, yh):
    return 4 * (yl ^ (x >> 1)) + 2 * (z0 ^ (x & 1)) + (co ^ yh)


def home_permutation():
    pairs = []
    for yl in range(2):
        for zh in range(4):
            for z0 in range(2):
                for x in range(4):
                    for yh in range(2):
                        for co in range(2):
                            half, right = zh >> 1, zh & 1
                            source = ((((yl * 4 + zh) * 2 + z0) * 4 + x) * 2 + yh) * 2 + co
                            row = 4 * x + 2 * yh + (co ^ half)
                            col = 2 * column_block(yl, z0, co, x, yh) + right
                            pairs.append((source, row * 16 + col))
    return pairs


def swapped_halves(tile):
    return pltpu.roll(tile.astype(jnp.float32), UNIT, 1)


def pack_kernel(place_ref, lengths_ref, slots_ref, out_ref, table_ref):
    replica = place_ref[0]
    begin = jnp.int32(0)
    for j in range(16):
        count = lengths_ref[replica, j] // UNIT
        for k in range(4):

            @pl.when(k < count)
            def _(begin=begin, j=j, k=k):
                table_ref[begin + k] = jnp.int32(4 * j + k)

        begin = begin + count
    lane = lax.broadcasted_iota(jnp.int32, slots_ref.shape[1:], 1)
    for d in range(16):
        left, right = table_ref[2 * d], table_ref[2 * d + 1]
        tile_l, tile_r = slots_ref[left // 2], slots_ref[right // 2]
        low = jnp.where(left % 2 == 0, tile_l.astype(jnp.float32), swapped_halves(tile_l))
        high = jnp.where(right % 2 == 1, tile_r.astype(jnp.float32), swapped_halves(tile_r))
        dense = jnp.where(lane < UNIT, low, high).astype(out_ref.dtype)
        block, part = d // 2, 128 * (d % 2)
        for x in range(4):
            for yh in range(2):
                for yl in range(2):
                    for z0 in range(2):
                        for co in range(2):
                            if column_block(yl, z0, co, x, yh) == block:
                                out_ref[yl, z0, 2 * x + yh, co, :, part : part + 128] = dense


def packed_columns(slots, lengths, place):
    tokens = slots.shape[1]
    smem = pl.BlockSpec(memory_space=pltpu.SMEM)
    vmem = pl.BlockSpec(memory_space=pltpu.VMEM)
    return pl.pallas_call(
        pack_kernel,
        out_shape=jax.ShapeDtypeStruct((2, 2, 8, 2, tokens, 256), slots.dtype),
        in_specs=[smem, smem, vmem],
        out_specs=vmem,
        scratch_shapes=[pltpu.SMEM((32,), jnp.int32)],
        cost_estimate=pl.CostEstimate(flops=1_000_000, bytes_accessed=5_000_000, transcendentals=0),
        name="pack",
    )(place, lengths, slots)


def unpack_kernel(place_ref, lengths_ref, weights_ref, out_ref, windows_ref):
    group = pl.program_id(0)
    replica = 8 * (group // 2) + 2 * place_ref[1] + group % 2
    zh, blocks, rows, width = weights_ref.shape
    lane = lax.broadcasted_iota(jnp.int32, (zh, rows, width), 2)

    @pl.when(group == 0)
    def _():
        def turned(t):
            tile = weights_ref[:, t].reshape(zh * rows, width)
            return pltpu.roll(tile.astype(jnp.float32), UNIT, 1).reshape(zh, rows, width)

        def window(t, low):
            high = turned(jnp.minimum(t + 1, blocks - 1))
            windows_ref[2 * t] = weights_ref[:, t]
            windows_ref[2 * t + 1] = jnp.where(lane < UNIT, low, high).astype(windows_ref.dtype)
            return high

        lax.fori_loop(0, blocks, window, turned(0))

    def slot(j, begin):
        count = lengths_ref[replica, j] // UNIT
        for k in range(2):
            value = windows_ref[jnp.minimum(begin + 2 * k, 2 * blocks - 1)]
            keep = lane < (count - 2 * k) * UNIT
            out_ref[j, :, :, width * k : width * (k + 1)] = jnp.where(keep, value, jnp.zeros_like(value))
        return begin + count

    lax.fori_loop(0, 16, slot, jnp.int32(0), unroll=True)


def slot_columns(weights, lengths, place):
    zh, blocks, rows, width = weights.shape
    smem = pl.BlockSpec(memory_space=pltpu.SMEM)
    return pl.pallas_call(
        unpack_kernel,
        out_shape=jax.ShapeDtypeStruct((64, zh, rows, 256), weights.dtype),
        grid=(4,),
        in_specs=[smem, smem, pl.BlockSpec((zh, blocks, rows, width), lambda g: (0, 0, 0, 0))],
        out_specs=pl.BlockSpec((16, zh, rows, 256), lambda g: (g, 0, 0, 0)),
        scratch_shapes=[pltpu.VMEM((2 * blocks, zh, rows, width), weights.dtype)],
        cost_estimate=pl.CostEstimate(flops=10_000_000, bytes_accessed=5_000_000, transcendentals=0),
        name="unpack",
    )(place, lengths, weights)


def ring(step):
    return [(k, (k + step) % 8) for k in range(8)]


def all_rows(weights):
    yl, z = lax.axis_index("yl"), lax.axis_index(Z)
    other = lax.ppermute(weights, "yl", SWAP)
    pair = jnp.stack([jnp.where(yl == 0, weights, other), jnp.where(yl == 0, other, weights)])
    out = jnp.zeros((2, 8, *weights.shape), weights.dtype)

    def put(out, piece, first, distance):
        return lax.dynamic_update_slice(out, piece[:, None], (first, (z + distance) % 8, 0, 0))

    out = put(out, pair, 0, 0)
    up, down = pair, pair
    for k in range(1, 4):
        up = lax.ppermute(up, Z, ring(1))
        down = lax.ppermute(down, Z, ring(-1))
        out = put(out, up, 0, 8 - k)
        out = put(out, down, 0, k)
    out = put(out, lax.ppermute(up[:1], Z, ring(1)), 0, 4)
    out = put(out, lax.ppermute(down[1:], Z, ring(-1)), 1, 4)
    return out.reshape(-1, weights.shape[1])


def product(tokens, dense):
    return lax.dot_general(tokens, dense, (((0,), (0,)), ((), ())), preferred_element_type=jnp.float32)


def on_device(tokens, grad_out, lengths, master, first, second):
    yl, z0 = lax.axis_index("yl"), lax.axis_index("z0")
    place = jnp.stack([lax.axis_index(REP), lax.axis_index("zh")]).astype(jnp.int32)
    token_count, slot_width = grad_out.shape
    half = token_count // 2

    across_y = lax.ppermute(tokens, "yl", SWAP)
    across_z = lax.ppermute(tokens, "z0", SWAP)
    across_top = lax.ppermute(across_y[:half], "z0", SWAP)
    across_bottom = lax.ppermute(across_z[half:], "yl", SWAP)
    own = [tokens, across_y, across_z, across_top, across_bottom]
    theirs = [lax.ppermute(part, "co", SWAP) for part in own]

    parts = jnp.swapaxes(grad_out.reshape(16, token_count // 16, 2, 128), 1, 2)
    slots = lax.all_to_all(parts, TP, split_axis=0, concat_axis=0, tiled=True)
    spread = packed_columns(slots.reshape(32, token_count // 16, 128), lengths, place)
    spread = spread.reshape(64, token_count // 16, 256)
    dense = lax.all_to_all(spread, GROUP, split_axis=0, concat_axis=0, tiled=True)
    dense = dense.reshape(4, token_count, 256)
    d00, d10, d01, d11 = (
        lax.dynamic_index_in_dim(dense, 2 * (yl ^ a) + (z0 ^ b), 0, False)
        for a, b in ((0, 0), (1, 0), (0, 1), (1, 1))
    )
    columns = [d00, d10, d01, d11[:half], d11[half:]]
    blocks = []
    for features in (own, theirs):
        total = sum(product(t, d) for t, d in zip(features, columns))
        total = total.astype(jnp.bfloat16)
        blocks += [total[:, :128], total[:, 128:]]
    arrived = lax.all_to_all(jnp.stack(blocks), "zh", split_axis=0, concat_axis=0, tiled=True)
    summed = jnp.sum(arrived.astype(jnp.float32), axis=0).astype(jnp.bfloat16)
    gradient = lax.ppermute(summed, AXES, home_permutation()).astype(jnp.float32)

    new_master, new_first, new_second = adam_update(master, first, second, gradient)
    weights = new_master.astype(jnp.bfloat16)

    rows = lax.all_to_all(weights.reshape(16, 32, 128), TP, split_axis=0, concat_axis=0, tiled=True)
    rows = jnp.broadcast_to(rows[None], (4, *rows.shape))
    rows = lax.all_to_all(rows, "zh", split_axis=0, concat_axis=0, tiled=True)
    outgoing = slot_columns(rows, lengths, place)
    incoming = lax.all_to_all(outgoing, GROUP, split_axis=0, concat_axis=0, tiled=True)
    slot_weights = incoming.reshape(2, 2, 16, 4, 32, slot_width).transpose(0, 3, 1, 2, 4, 5)
    slot_weights = slot_weights.reshape(1, -1, slot_width)
    healthy = all_rows(weights)
    return (new_master, new_first, new_second, healthy, slot_weights)


def solution(mesh):
    torus = Mesh(mesh.devices.reshape(2, 4, 2, 4, 2, 2), AXES)
    placed = (P(REP, TP), P(REP, TP), P(), P(REP, TP), P(REP, TP), P(REP, TP))

    return jax.shard_map(
        on_device,
        mesh=torus,
        in_specs=placed,
        out_specs=(P(REP, TP), P(REP, TP), P(REP, TP), P(None, TP), P(REP, None, TP)),
        check_vma=False,
    )
```

```python
import jax
import jax.numpy as jnp
from jax import lax
from jax.experimental import pallas as pl
from jax.experimental.pallas import tpu as pltpu
from jax.sharding import Mesh
from jax.sharding import PartitionSpec as P

STEP = 1000
UNIT = 64
AXES = ("yl", "zh", "z0", "x", "yh", "co")
REP = ("yl", "zh", "z0")
TP = ("x", "yh", "co")
Z = ("zh", "z0")
PAIR = ("z0", "x", "yh", "co")
GROUP = ("yl", "z0", "x", "yh", "co")
SUM = ("yl", "zh")
SWAP = [(0, 1), (1, 0)]

decay_first = 0.9
decay_second = 0.999
learning_rate = 0.02
weight_decay = 0.1
epsilon = 1e-08


def adam_update(master, first, second, gradient):
    scale_first = 1.0 - decay_first**STEP
    scale_second = 1.0 - decay_second**STEP
    new_first = decay_first * first + (1.0 - decay_first) * gradient
    new_second = decay_second * second + (1.0 - decay_second) * gradient * gradient
    direction = new_first / scale_first / (jnp.sqrt(new_second / scale_second) + epsilon)
    new_master = master - learning_rate * (direction + weight_decay * master)
    return (new_master, new_first, new_second)


def sum_block(yl, zh):
    return zh // 2, 2 * yl + zh % 2


def column_block(z0, co, x, yh):
    return 2 * (z0 ^ (x % 2)) + (co ^ (x % 2) ^ yh)


def home_permutation():
    pairs = []
    for yl in range(2):
        for zh in range(4):
            for z0 in range(2):
                for x in range(4):
                    for yh in range(2):
                        for co in range(2):
                            half, part = sum_block(yl, zh)
                            source = ((((yl * 4 + zh) * 2 + z0) * 4 + x) * 2 + yh) * 2 + co
                            row = 4 * x + 2 * yh + (co ^ half)
                            col = 4 * column_block(z0, co, x, yh) + part
                            pairs.append((source, row * 16 + col))
    return pairs


def swapped_halves(tile):
    return pltpu.roll(tile.astype(jnp.float32), UNIT, 1)


def pack_kernel(place_ref, lengths_ref, slots_ref, out_ref, table_ref):
    replica = place_ref[0]
    begin = jnp.int32(0)
    for j in range(16):
        count = lengths_ref[replica, j] // UNIT
        for k in range(4):

            @pl.when(k < count)
            def _(begin=begin, j=j, k=k):
                table_ref[begin + k] = jnp.int32(4 * j + k)

        begin = begin + count
    lane = lax.broadcasted_iota(jnp.int32, (slots_ref.shape[1], 128), 1)

    def tile_of(unit):
        return slots_ref[unit // 4, :, pl.ds(pl.multiple_of((unit // 2) % 2 * 128, 128), 128)]

    for d in range(16):
        left, right = table_ref[2 * d], table_ref[2 * d + 1]
        tile_l, tile_r = tile_of(left), tile_of(right)
        low = jnp.where(left % 2 == 0, tile_l.astype(jnp.float32), swapped_halves(tile_l))
        high = jnp.where(right % 2 == 1, tile_r.astype(jnp.float32), swapped_halves(tile_r))
        dense = jnp.where(lane < UNIT, low, high).astype(out_ref.dtype)
        block, part = d // 4, 128 * (d % 4)
        for x in range(4):
            for yh in range(2):
                for z0 in range(2):
                    for co in range(2):
                        if column_block(z0, co, x, yh) == block:
                            out_ref[z0, 2 * x + yh, co, :, part : part + 128] = dense


def packed_columns(slots, lengths, place):
    tokens = slots.shape[1]
    smem = pl.BlockSpec(memory_space=pltpu.SMEM)
    vmem = pl.BlockSpec(memory_space=pltpu.VMEM)
    return pl.pallas_call(
        pack_kernel,
        out_shape=jax.ShapeDtypeStruct((2, 8, 2, tokens, 512), slots.dtype),
        in_specs=[smem, smem, vmem],
        out_specs=vmem,
        scratch_shapes=[pltpu.SMEM((32,), jnp.int32)],
        cost_estimate=pl.CostEstimate(flops=1_000_000, bytes_accessed=5_000_000, transcendentals=0),
        name="pack",
    )(place, lengths, slots)


def unpack_kernel(place_ref, lengths_ref, weights_ref, out_ref, windows_ref):
    group = pl.program_id(0)
    replica = 8 * (group // 2) + 2 * place_ref[1] + group % 2
    zh, blocks, rows, width = weights_ref.shape
    lane = lax.broadcasted_iota(jnp.int32, (zh, rows, width), 2)

    @pl.when(group == 0)
    def _():
        def turned(t):
            tile = weights_ref[:, t].reshape(zh * rows, width)
            return pltpu.roll(tile.astype(jnp.float32), UNIT, 1).reshape(zh, rows, width)

        def window(t, low):
            high = turned(jnp.minimum(t + 1, blocks - 1))
            windows_ref[2 * t] = weights_ref[:, t]
            windows_ref[2 * t + 1] = jnp.where(lane < UNIT, low, high).astype(windows_ref.dtype)
            return high

        lax.fori_loop(0, blocks, window, turned(0))

    def slot(j, begin):
        count = lengths_ref[replica, j] // UNIT
        for k in range(2):
            value = windows_ref[jnp.minimum(begin + 2 * k, 2 * blocks - 1)]
            keep = lane < (count - 2 * k) * UNIT
            out_ref[j, :, :, width * k : width * (k + 1)] = jnp.where(keep, value, jnp.zeros_like(value))
        return begin + count

    lax.fori_loop(0, 16, slot, jnp.int32(0), unroll=True)


def slot_columns(weights, lengths, place):
    zh, blocks, rows, width = weights.shape
    smem = pl.BlockSpec(memory_space=pltpu.SMEM)
    return pl.pallas_call(
        unpack_kernel,
        out_shape=jax.ShapeDtypeStruct((64, zh, rows, 256), weights.dtype),
        grid=(4,),
        in_specs=[smem, smem, pl.BlockSpec((zh, blocks, rows, width), lambda g: (0, 0, 0, 0))],
        out_specs=pl.BlockSpec((16, zh, rows, 256), lambda g: (g, 0, 0, 0)),
        scratch_shapes=[pltpu.VMEM((2 * blocks, zh, rows, width), weights.dtype)],
        cost_estimate=pl.CostEstimate(flops=10_000_000, bytes_accessed=5_000_000, transcendentals=0),
        name="unpack",
    )(place, lengths, weights)


def ring(step):
    return [(k, (k + step) % 8) for k in range(8)]


def all_rows(weights):
    yl, z = lax.axis_index("yl"), lax.axis_index(Z)
    other = lax.ppermute(weights, "yl", SWAP)
    pair = jnp.stack([jnp.where(yl == 0, weights, other), jnp.where(yl == 0, other, weights)])
    out = jnp.zeros((2, 8, *weights.shape), weights.dtype)

    def put(out, piece, first, distance):
        return lax.dynamic_update_slice(out, piece[:, None], (first, (z + distance) % 8, 0, 0))

    out = put(out, pair, 0, 0)
    up, down = pair, pair
    for k in range(1, 4):
        up = lax.ppermute(up, Z, ring(1))
        down = lax.ppermute(down, Z, ring(-1))
        out = put(out, up, 0, 8 - k)
        out = put(out, down, 0, k)
    up = lax.ppermute(up[:1], Z, ring(1))
    down = lax.ppermute(down[1:], Z, ring(-1))
    out = put(out, up, 0, 4)
    out = put(out, down, 1, 4)
    return out.reshape(-1, weights.shape[1])


def product(tokens, dense):
    return lax.dot_general(tokens, dense, (((0,), (0,)), ((), ())), preferred_element_type=jnp.float32)


def on_device(tokens, grad_out, lengths, master, first, second):
    z0 = lax.axis_index("z0")
    place = jnp.stack([lax.axis_index(REP), lax.axis_index("zh")]).astype(jnp.int32)
    token_count, slot_width = grad_out.shape

    across = lax.ppermute(tokens, "z0", SWAP)
    own = [tokens, across]
    theirs = [lax.ppermute(part, "co", SWAP) for part in own]

    parts = grad_out.reshape(16, token_count // 16, slot_width)
    slots = lax.all_to_all(parts, TP, split_axis=0, concat_axis=0, tiled=True)
    spread = packed_columns(slots, lengths, place).reshape(32, token_count // 16, 512)
    dense = lax.all_to_all(spread, PAIR, split_axis=0, concat_axis=0, tiled=True)
    dense = dense.reshape(2, token_count, 512)
    columns = [lax.dynamic_index_in_dim(dense, z0 ^ k, 0, False) for k in range(2)]
    totals = [
        sum(product(t, d) for t, d in zip(features, columns)).astype(jnp.bfloat16)
        for features in (own, theirs)
    ]
    blocks = []
    for yl in range(2):
        for zh in range(4):
            half, part = sum_block(yl, zh)
            blocks.append(totals[half][:, 128 * part : 128 * (part + 1)])
    arrived = lax.all_to_all(jnp.stack(blocks), SUM, split_axis=0, concat_axis=0, tiled=True)
    summed = jnp.sum(arrived.astype(jnp.float32), axis=0).astype(jnp.bfloat16)
    gradient = lax.ppermute(summed, AXES, home_permutation()).astype(jnp.float32)

    new_master, new_first, new_second = adam_update(master, first, second, gradient)
    weights = new_master.astype(jnp.bfloat16)

    rows = lax.all_to_all(weights.reshape(16, 32, 128), TP, split_axis=0, concat_axis=0, tiled=True)
    rows = jnp.broadcast_to(rows[None], (4, *rows.shape))
    rows = lax.all_to_all(rows, "zh", split_axis=0, concat_axis=0, tiled=True)
    outgoing = slot_columns(rows, lengths, place)
    incoming = lax.all_to_all(outgoing, GROUP, split_axis=0, concat_axis=0, tiled=True)
    slot_weights = incoming.reshape(2, 2, 16, 4, 32, slot_width).transpose(0, 3, 1, 2, 4, 5)
    slot_weights = slot_weights.reshape(1, -1, slot_width)
    healthy = all_rows(weights)
    return (new_master, new_first, new_second, healthy, slot_weights)


def solution(mesh):
    torus = Mesh(mesh.devices.reshape(2, 4, 2, 4, 2, 2), AXES)
    placed = (P(REP, TP), P(REP, TP), P(), P(REP, TP), P(REP, TP), P(REP, TP))

    return jax.shard_map(
        on_device,
        mesh=torus,
        in_specs=placed,
        out_specs=(P(REP, TP), P(REP, TP), P(REP, TP), P(None, TP), P(REP, None, TP)),
        check_vma=False,
    )
```

```python
import jax
import jax.numpy as jnp
from jax import lax
from jax.experimental import pallas as pl
from jax.experimental.pallas import tpu as pltpu
from jax.sharding import Mesh
from jax.sharding import PartitionSpec as P

STEP = 1000
UNIT = 64
AXES = ("yl", "zh", "z0", "x", "yh", "co")
REP = ("yl", "zh", "z0")
TP = ("x", "yh", "co")
Z = ("zh", "z0")
PAIR = ("z0", "x", "yh", "co")
GROUP = ("yl", "z0", "x", "yh", "co")
SUM = ("yl", "zh")
SWAP = [(0, 1), (1, 0)]

decay_first = 0.9
decay_second = 0.999
learning_rate = 0.02
weight_decay = 0.1
epsilon = 1e-08


def adam_update(master, first, second, gradient):
    scale_first = 1.0 - decay_first**STEP
    scale_second = 1.0 - decay_second**STEP
    new_first = decay_first * first + (1.0 - decay_first) * gradient
    new_second = decay_second * second + (1.0 - decay_second) * gradient * gradient
    direction = new_first / scale_first / (jnp.sqrt(new_second / scale_second) + epsilon)
    new_master = master - learning_rate * (direction + weight_decay * master)
    return (new_master, new_first, new_second)


def sum_block(yl, zh):
    return zh // 2, 2 * yl + zh % 2


def column_block(z0, co, x, yh):
    return 2 * (z0 ^ (x % 2)) + (co ^ (x % 2) ^ yh)


def home_permutation():
    pairs = []
    for yl in range(2):
        for zh in range(4):
            for z0 in range(2):
                for x in range(4):
                    for yh in range(2):
                        for co in range(2):
                            half, part = sum_block(yl, zh)
                            source = ((((yl * 4 + zh) * 2 + z0) * 4 + x) * 2 + yh) * 2 + co
                            row = 4 * x + 2 * yh + (co ^ half)
                            col = 4 * column_block(z0, co, x, yh) + part
                            pairs.append((source, row * 16 + col))
    return pairs


def swapped_halves(tile):
    return pltpu.roll(tile.astype(jnp.float32), UNIT, 1)


def pack_kernel(place_ref, lengths_ref, slots_ref, out_ref, table_ref):
    replica = place_ref[0]
    begin = jnp.int32(0)
    for j in range(16):
        count = lengths_ref[replica, j] // UNIT
        for k in range(4):

            @pl.when(k < count)
            def _(begin=begin, j=j, k=k):
                table_ref[begin + k] = jnp.int32(4 * j + k)

        begin = begin + count
    lane = lax.broadcasted_iota(jnp.int32, (slots_ref.shape[1], 128), 1)

    def tile_of(unit):
        return slots_ref[unit // 4, :, pl.ds(pl.multiple_of((unit // 2) % 2 * 128, 128), 128)]

    for d in range(16):
        left, right = table_ref[2 * d], table_ref[2 * d + 1]
        tile_l, tile_r = tile_of(left), tile_of(right)
        low = jnp.where(left % 2 == 0, tile_l.astype(jnp.float32), swapped_halves(tile_l))
        high = jnp.where(right % 2 == 1, tile_r.astype(jnp.float32), swapped_halves(tile_r))
        dense = jnp.where(lane < UNIT, low, high).astype(out_ref.dtype)
        block, part = d // 4, 128 * (d % 4)
        for x in range(4):
            for yh in range(2):
                for z0 in range(2):
                    for co in range(2):
                        if column_block(z0, co, x, yh) == block:
                            out_ref[z0, 2 * x + yh, co, :, part : part + 128] = dense


def packed_columns(slots, lengths, place):
    tokens = slots.shape[1]
    smem = pl.BlockSpec(memory_space=pltpu.SMEM)
    vmem = pl.BlockSpec(memory_space=pltpu.VMEM)
    return pl.pallas_call(
        pack_kernel,
        out_shape=jax.ShapeDtypeStruct((2, 8, 2, tokens, 512), slots.dtype),
        in_specs=[smem, smem, vmem],
        out_specs=vmem,
        scratch_shapes=[pltpu.SMEM((32,), jnp.int32)],
        cost_estimate=pl.CostEstimate(flops=1_000_000, bytes_accessed=5_000_000, transcendentals=0),
        name="pack",
    )(place, lengths, slots)


def unpack_kernel(place_ref, lengths_ref, weights_ref, out_ref, windows_ref):
    group = pl.program_id(0)
    replica = 8 * (group // 2) + 2 * place_ref[1] + group % 2
    pieces, blocks, rows, width = weights_ref.shape
    lane = lax.broadcasted_iota(jnp.int32, (pieces, rows, width), 2)

    @pl.when(group == 0)
    def _():
        def turned(t):
            tile = weights_ref[:, t].reshape(pieces * rows, width)
            return pltpu.roll(tile.astype(jnp.float32), UNIT, 1).reshape(pieces, rows, width)

        def window(t, low):
            high = turned(jnp.minimum(t + 1, blocks - 1))
            windows_ref[2 * t] = weights_ref[:, t]
            windows_ref[2 * t + 1] = jnp.where(lane < UNIT, low, high).astype(windows_ref.dtype)
            return high

        lax.fori_loop(0, blocks, window, turned(0))

    def slot(j, begin):
        count = lengths_ref[replica, j] // UNIT
        for k in range(2):
            value = windows_ref[jnp.minimum(begin + 2 * k, 2 * blocks - 1)]
            keep = lane < (count - 2 * k) * UNIT
            out_ref[j, :, :, width * k : width * (k + 1)] = jnp.where(keep, value, jnp.zeros_like(value))
        return begin + count

    lax.fori_loop(0, 16, slot, jnp.int32(0), unroll=True)


def slot_columns(weights, lengths, place):
    pieces, blocks, rows, width = weights.shape
    smem = pl.BlockSpec(memory_space=pltpu.SMEM)
    return pl.pallas_call(
        unpack_kernel,
        out_shape=jax.ShapeDtypeStruct((64, pieces, rows, 256), weights.dtype),
        grid=(4,),
        in_specs=[smem, smem, pl.BlockSpec((pieces, blocks, rows, width), lambda g: (0, 0, 0, 0))],
        out_specs=pl.BlockSpec((16, pieces, rows, 256), lambda g: (g, 0, 0, 0)),
        scratch_shapes=[pltpu.VMEM((2 * blocks, pieces, rows, width), weights.dtype)],
        cost_estimate=pl.CostEstimate(flops=3_000_000 * pieces, bytes_accessed=1_300_000 * pieces, transcendentals=0),
        name="unpack",
    )(place, lengths, weights)


def ring(step):
    return [(k, (k + step) % 8) for k in range(8)]


def all_rows(weights):
    yl, z = lax.axis_index("yl"), lax.axis_index(Z)
    other = lax.ppermute(weights, "yl", SWAP)
    pair = jnp.stack([jnp.where(yl == 0, weights, other), jnp.where(yl == 0, other, weights)])
    out = jnp.zeros((2, 8, *weights.shape), weights.dtype)

    def put(out, piece, first, distance):
        return lax.dynamic_update_slice(out, piece[:, None], (first, (z + distance) % 8, 0, 0))

    out = put(out, pair, 0, 0)
    up, down = pair, pair
    for k in range(1, 4):
        up = lax.ppermute(up, Z, ring(1))
        down = lax.ppermute(down, Z, ring(-1))
        out = put(out, up, 0, 8 - k)
        out = put(out, down, 0, k)
    up = lax.ppermute(up[:1], Z, ring(1))
    down = lax.ppermute(down[1:], Z, ring(-1))
    out = put(out, up, 0, 4)
    out = put(out, down, 1, 4)
    return out.reshape(-1, weights.shape[1])


def product(tokens, dense):
    return lax.dot_general(tokens, dense, (((0,), (0,)), ((), ())), preferred_element_type=jnp.float32)


def on_device(tokens, grad_out, lengths, master, first, second):
    z0 = lax.axis_index("z0")
    place = jnp.stack([lax.axis_index(REP), lax.axis_index("zh")]).astype(jnp.int32)
    token_count, slot_width = grad_out.shape

    across = lax.ppermute(tokens, "z0", SWAP)
    own = [tokens, across]
    theirs = [lax.ppermute(part, "co", SWAP) for part in own]

    parts = grad_out.reshape(16, token_count // 16, slot_width)
    slots = lax.all_to_all(parts, TP, split_axis=0, concat_axis=0, tiled=True)
    spread = packed_columns(slots, lengths, place).reshape(32, token_count // 16, 512)
    dense = lax.all_to_all(spread, PAIR, split_axis=0, concat_axis=0, tiled=True)
    dense = dense.reshape(2, token_count, 512)
    columns = [lax.dynamic_index_in_dim(dense, z0 ^ k, 0, False) for k in range(2)]
    totals = [
        sum(product(t, d) for t, d in zip(features, columns)).astype(jnp.bfloat16)
        for features in (own, theirs)
    ]
    blocks = []
    for yl in range(2):
        for zh in range(4):
            half, part = sum_block(yl, zh)
            blocks.append(totals[half][:, 128 * part : 128 * (part + 1)])
    arrived = lax.all_to_all(jnp.stack(blocks), SUM, split_axis=0, concat_axis=0, tiled=True)
    summed = jnp.sum(arrived.astype(jnp.float32), axis=0).astype(jnp.bfloat16)
    gradient = lax.ppermute(summed, AXES, home_permutation()).astype(jnp.float32)

    new_master, new_first, new_second = adam_update(master, first, second, gradient)
    weights = new_master.astype(jnp.bfloat16)

    rows = lax.all_to_all(weights.reshape(16, 32, 128), TP, split_axis=0, concat_axis=0, tiled=True)
    others = [lax.ppermute(rows, "zh", [(k, (k + step) % 4) for k in range(4)]) for step in (3, 2, 1)]
    zh = lax.axis_index("zh")
    slot_weights = jnp.zeros((2, 4, 2, 16, 32, slot_width), weights.dtype)
    distance = 0
    for pieces in (rows[None], jnp.stack(others)):
        outgoing = slot_columns(pieces, lengths, place)
        incoming = lax.all_to_all(outgoing, GROUP, split_axis=0, concat_axis=0, tiled=True)
        incoming = incoming.reshape(2, 2, 16, -1, 32, slot_width).transpose(0, 3, 1, 2, 4, 5)
        for piece in range(incoming.shape[1]):
            slot_weights = lax.dynamic_update_slice(
                slot_weights, incoming[:, piece : piece + 1], (0, (zh + distance) % 4, 0, 0, 0, 0)
            )
            distance += 1
    slot_weights = slot_weights.reshape(1, -1, slot_width)
    healthy = all_rows(weights)
    return (new_master, new_first, new_second, healthy, slot_weights)


def solution(mesh):
    torus = Mesh(mesh.devices.reshape(2, 4, 2, 4, 2, 2), AXES)
    placed = (P(REP, TP), P(REP, TP), P(), P(REP, TP), P(REP, TP), P(REP, TP))

    return jax.shard_map(
        on_device,
        mesh=torus,
        in_specs=placed,
        out_specs=(P(REP, TP), P(REP, TP), P(REP, TP), P(None, TP), P(REP, None, TP)),
        check_vma=False,
    )
```

```python
import jax
import jax.numpy as jnp
from jax import lax
from jax.experimental import pallas as pl
from jax.experimental.pallas import tpu as pltpu
from jax.experimental.layout import Layout, with_layout_constraint
from jax.sharding import Mesh
from jax.sharding import PartitionSpec as P

STEP = 1000
UNIT = 64
AXES = ("yl", "zh", "z0", "x", "yh", "co")
REP = ("yl", "zh", "z0")
TP = ("x", "yh", "co")
Z = ("zh", "z0")
PAIR = ("z0", "x", "yh", "co")
GROUP = ("yl", "z0", "x", "yh", "co")
SUM = ("yl", "zh")
SWAP = [(0, 1), (1, 0)]

decay_first = 0.9
decay_second = 0.999
learning_rate = 0.02
weight_decay = 0.1
epsilon = 1e-08


def adam_update(master, first, second, gradient):
    scale_first = 1.0 - decay_first**STEP
    scale_second = 1.0 - decay_second**STEP
    new_first = decay_first * first + (1.0 - decay_first) * gradient
    new_second = decay_second * second + (1.0 - decay_second) * gradient * gradient
    direction = new_first / scale_first / (jnp.sqrt(new_second / scale_second) + epsilon)
    new_master = master - learning_rate * (direction + weight_decay * master)
    return (new_master, new_first, new_second)


def sum_block(yl, zh):
    return zh // 2, 2 * yl + zh % 2


def column_block(z0, co, x, yh):
    return 2 * (z0 ^ (x % 2)) + (co ^ (x % 2) ^ yh)


def home_permutation():
    pairs = []
    for yl in range(2):
        for zh in range(4):
            for z0 in range(2):
                for x in range(4):
                    for yh in range(2):
                        for co in range(2):
                            half, part = sum_block(yl, zh)
                            source = ((((yl * 4 + zh) * 2 + z0) * 4 + x) * 2 + yh) * 2 + co
                            row = 4 * x + 2 * yh + (co ^ half)
                            col = 4 * column_block(z0, co, x, yh) + part
                            pairs.append((source, row * 16 + col))
    return pairs


def swapped_halves(tile):
    return pltpu.roll(tile.astype(jnp.float32), UNIT, 1)


def pack_kernel(place_ref, lengths_ref, slots_ref, out_ref, table_ref):
    replica = place_ref[0]
    begin = jnp.int32(0)
    for j in range(16):
        count = lengths_ref[replica, j] // UNIT
        for k in range(4):

            @pl.when(k < count)
            def _(begin=begin, j=j, k=k):
                table_ref[begin + k] = jnp.int32(4 * j + k)

        begin = begin + count
    lane = lax.broadcasted_iota(jnp.int32, (slots_ref.shape[1], 128), 1)

    def tile_of(unit):
        return slots_ref[unit // 4, :, pl.ds(pl.multiple_of((unit // 2) % 2 * 128, 128), 128)]

    for d in range(16):
        left, right = table_ref[2 * d], table_ref[2 * d + 1]
        tile_l, tile_r = tile_of(left), tile_of(right)
        low = jnp.where(left % 2 == 0, tile_l.astype(jnp.float32), swapped_halves(tile_l))
        high = jnp.where(right % 2 == 1, tile_r.astype(jnp.float32), swapped_halves(tile_r))
        dense = jnp.where(lane < UNIT, low, high).astype(out_ref.dtype)
        block, part = d // 4, 128 * (d % 4)
        for x in range(4):
            for yh in range(2):
                for z0 in range(2):
                    for co in range(2):
                        if column_block(z0, co, x, yh) == block:
                            out_ref[z0, 2 * x + yh, co, :, part : part + 128] = dense


def packed_columns(slots, lengths, place):
    tokens = slots.shape[1]
    smem = pl.BlockSpec(memory_space=pltpu.SMEM)
    vmem = pl.BlockSpec(memory_space=pltpu.VMEM)
    return pl.pallas_call(
        pack_kernel,
        out_shape=jax.ShapeDtypeStruct((2, 8, 2, tokens, 512), slots.dtype),
        in_specs=[smem, smem, vmem],
        out_specs=vmem,
        scratch_shapes=[pltpu.SMEM((32,), jnp.int32)],
        cost_estimate=pl.CostEstimate(flops=1_000_000, bytes_accessed=5_000_000, transcendentals=0),
        name="pack",
    )(place, lengths, slots)


def unpack_kernel(place_ref, lengths_ref, weights_ref, out_ref, windows_ref):
    group = pl.program_id(0)
    replica = 8 * (group // 2) + 2 * place_ref[1] + group % 2
    pieces, blocks, rows, width = weights_ref.shape
    lane = lax.broadcasted_iota(jnp.int32, (pieces, rows, width), 2)

    @pl.when(group == 0)
    def _():
        def turned(t):
            tile = weights_ref[:, t].reshape(pieces * rows, width)
            return pltpu.roll(tile.astype(jnp.float32), UNIT, 1).reshape(pieces, rows, width)

        def window(t, low):
            high = turned(jnp.minimum(t + 1, blocks - 1))
            windows_ref[2 * t] = weights_ref[:, t]
            windows_ref[2 * t + 1] = jnp.where(lane < UNIT, low, high).astype(windows_ref.dtype)
            return high

        lax.fori_loop(0, blocks, window, turned(0), unroll=True)

    def slot(j, begin):
        count = lengths_ref[replica, j] // UNIT
        for k in range(2):
            value = windows_ref[jnp.minimum(begin + 2 * k, 2 * blocks - 1)]
            keep = lane < (count - 2 * k) * UNIT
            out_ref[j, :, :, width * k : width * (k + 1)] = jnp.where(keep, value, jnp.zeros_like(value))
        return begin + count

    lax.fori_loop(0, 16, slot, jnp.int32(0), unroll=True)


def slot_columns(weights, lengths, place):
    pieces, blocks, rows, width = weights.shape
    smem = pl.BlockSpec(memory_space=pltpu.SMEM)
    return pl.pallas_call(
        unpack_kernel,
        out_shape=jax.ShapeDtypeStruct((64, pieces, rows, 256), weights.dtype),
        grid=(4,),
        in_specs=[smem, smem, pl.BlockSpec((pieces, blocks, rows, width), lambda g: (0, 0, 0, 0))],
        out_specs=pl.BlockSpec((16, pieces, rows, 256), lambda g: (g, 0, 0, 0)),
        scratch_shapes=[pltpu.VMEM((2 * blocks, pieces, rows, width), weights.dtype)],
        cost_estimate=pl.CostEstimate(flops=3_000_000 * pieces, bytes_accessed=1_300_000 * pieces, transcendentals=0),
        name="unpack",
    )(place, lengths, weights)


def ring(step):
    return [(k, (k + step) % 8) for k in range(8)]


def all_rows(weights):
    yl, z = lax.axis_index("yl"), lax.axis_index(Z)
    other = lax.ppermute(weights, "yl", SWAP)
    pair = jnp.stack([jnp.where(yl == 0, weights, other), jnp.where(yl == 0, other, weights)])
    out = jnp.zeros((2, 8, *weights.shape), weights.dtype)

    def put(out, piece, first, distance):
        return lax.dynamic_update_slice(out, piece[:, None], (first, (z + distance) % 8, 0, 0))

    out = put(out, pair, 0, 0)
    up, down = pair, pair
    for k in range(1, 4):
        up = lax.ppermute(up, Z, ring(1))
        down = lax.ppermute(down, Z, ring(-1))
        out = put(out, up, 0, 8 - k)
        out = put(out, down, 0, k)
    up = lax.ppermute(up[:1], Z, ring(1))
    down = lax.ppermute(down[1:], Z, ring(-1))
    out = put(out, up, 0, 4)
    out = put(out, down, 1, 4)
    return out.reshape(-1, weights.shape[1])


def product(tokens, dense):
    return lax.dot_general(tokens, dense, (((0,), (0,)), ((), ())), preferred_element_type=jnp.float32)


def on_device(tokens, grad_out, lengths, master, first, second):
    z0 = lax.axis_index("z0")
    place = jnp.stack([lax.axis_index(REP), lax.axis_index("zh")]).astype(jnp.int32)
    token_count, slot_width = grad_out.shape

    across = lax.ppermute(tokens, "z0", SWAP)
    own = [tokens, across]
    theirs = [lax.ppermute(part, "co", SWAP) for part in own]

    parts = grad_out.reshape(16, token_count // 16, slot_width)
    slots = lax.all_to_all(parts, TP, split_axis=0, concat_axis=0, tiled=True)
    spread = packed_columns(slots, lengths, place).reshape(32, token_count // 16, 512)
    dense = lax.all_to_all(spread, PAIR, split_axis=0, concat_axis=0, tiled=True)
    dense = dense.reshape(2, token_count, 512)
    columns = [lax.dynamic_index_in_dim(dense, z0 ^ k, 0, False) for k in range(2)]
    totals = [
        sum(product(t, d) for t, d in zip(features, columns)).astype(jnp.bfloat16)
        for features in (own, theirs)
    ]
    blocks = []
    for yl in range(2):
        for zh in range(4):
            half, part = sum_block(yl, zh)
            blocks.append(totals[half][:, 128 * part : 128 * (part + 1)])
    arrived = lax.all_to_all(jnp.stack(blocks), SUM, split_axis=0, concat_axis=0, tiled=True)
    summed = jnp.sum(arrived.astype(jnp.float32), axis=0).astype(jnp.bfloat16)
    gradient = lax.ppermute(summed, AXES, home_permutation())
    gradient = with_layout_constraint(gradient, Layout(major_to_minor=(0, 1))).astype(jnp.float32)

    new_master, new_first, new_second = adam_update(master, first, second, gradient)
    weights = new_master.astype(jnp.bfloat16)

    rows = lax.all_to_all(weights.reshape(16, 32, 128), TP, split_axis=0, concat_axis=0, tiled=True)
    others = [lax.ppermute(rows, "zh", [(k, (k + step) % 4) for k in range(4)]) for step in (3, 2, 1)]
    zh = lax.axis_index("zh")
    slot_weights = jnp.zeros((2, 4, 2, 16, 32, slot_width), weights.dtype)
    distance = 0
    for pieces in (rows[None], jnp.stack(others)):
        outgoing = slot_columns(pieces, lengths, place)
        incoming = lax.all_to_all(outgoing, GROUP, split_axis=0, concat_axis=0, tiled=True)
        incoming = incoming.reshape(2, 2, 16, -1, 32, slot_width).transpose(0, 3, 1, 2, 4, 5)
        for piece in range(incoming.shape[1]):
            slot_weights = lax.dynamic_update_slice(
                slot_weights, incoming[:, piece : piece + 1], (0, (zh + distance) % 4, 0, 0, 0, 0)
            )
            distance += 1
    slot_weights = slot_weights.reshape(1, -1, slot_width)
    healthy = all_rows(weights)
    return (new_master, new_first, new_second, healthy, slot_weights)


def solution(mesh):
    torus = Mesh(mesh.devices.reshape(2, 4, 2, 4, 2, 2), AXES)
    placed = (P(REP, TP), P(REP, TP), P(), P(REP, TP), P(REP, TP), P(REP, TP))

    return jax.shard_map(
        on_device,
        mesh=torus,
        in_specs=placed,
        out_specs=(P(REP, TP), P(REP, TP), P(REP, TP), P(None, TP), P(REP, None, TP)),
        check_vma=False,
    )
```

```python
import jax
import jax.numpy as jnp
from jax import lax
from jax.experimental import pallas as pl
from jax.experimental.pallas import tpu as pltpu
from jax.experimental.layout import Layout, with_layout_constraint
from jax.sharding import Mesh
from jax.sharding import PartitionSpec as P

STEP = 1000
UNIT = 64
AXES = ("yl", "zh", "z0", "x", "yh", "co")
REP = ("yl", "zh", "z0")
TP = ("x", "yh", "co")
Z = ("zh", "z0")
PAIR = ("z0", "x", "yh", "co")
GROUP = ("yl", "z0", "x", "yh", "co")
SUM = ("yl", "zh")
SWAP = [(0, 1), (1, 0)]

decay_first = 0.9
decay_second = 0.999
learning_rate = 0.02
weight_decay = 0.1
epsilon = 1e-08


def adam_update(master, first, second, gradient):
    scale_first = 1.0 - decay_first**STEP
    scale_second = 1.0 - decay_second**STEP
    new_first = decay_first * first + (1.0 - decay_first) * gradient
    new_second = decay_second * second + (1.0 - decay_second) * gradient * gradient
    direction = new_first / scale_first / (jnp.sqrt(new_second / scale_second) + epsilon)
    new_master = master - learning_rate * (direction + weight_decay * master)
    return (new_master, new_first, new_second)


def sum_block(yl, zh):
    return zh // 2, 2 * yl + zh % 2


def column_block(z0, co, x, yh):
    return 2 * (z0 ^ (x % 2)) + (co ^ (x % 2) ^ yh)


def home_permutation():
    pairs = []
    for yl in range(2):
        for zh in range(4):
            for z0 in range(2):
                for x in range(4):
                    for yh in range(2):
                        for co in range(2):
                            half, part = sum_block(yl, zh)
                            source = ((((yl * 4 + zh) * 2 + z0) * 4 + x) * 2 + yh) * 2 + co
                            row = 4 * x + 2 * yh + (co ^ half)
                            col = 4 * column_block(z0, co, x, yh) + part
                            pairs.append((source, row * 16 + col))
    return pairs


def swapped_halves(tile):
    return pltpu.roll(tile.astype(jnp.float32), UNIT, 1)


def pack_kernel(place_ref, lengths_ref, slots_ref, out_ref, table_ref):
    replica = place_ref[0]
    begin = jnp.int32(0)
    for j in range(16):
        count = lengths_ref[replica, j] // UNIT
        for k in range(4):

            @pl.when(k < count)
            def _(begin=begin, j=j, k=k):
                table_ref[begin + k] = jnp.int32(4 * j + k)

        begin = begin + count
    lane = lax.broadcasted_iota(jnp.int32, (slots_ref.shape[1], 128), 1)

    def tile_of(unit):
        return slots_ref[unit // 4, :, pl.ds(pl.multiple_of((unit // 2) % 2 * 128, 128), 128)]

    for d in range(16):
        left, right = table_ref[2 * d], table_ref[2 * d + 1]
        tile_l, tile_r = tile_of(left), tile_of(right)
        low = jnp.where(left % 2 == 0, tile_l.astype(jnp.float32), swapped_halves(tile_l))
        high = jnp.where(right % 2 == 1, tile_r.astype(jnp.float32), swapped_halves(tile_r))
        dense = jnp.where(lane < UNIT, low, high).astype(out_ref.dtype)
        block, part = d // 4, 128 * (d % 4)
        for x in range(4):
            for yh in range(2):
                for z0 in range(2):
                    for co in range(2):
                        if column_block(z0, co, x, yh) == block:
                            out_ref[z0, 2 * x + yh, co, :, part : part + 128] = dense


def packed_columns(slots, lengths, place):
    tokens = slots.shape[1]
    smem = pl.BlockSpec(memory_space=pltpu.SMEM)
    vmem = pl.BlockSpec(memory_space=pltpu.VMEM)
    return pl.pallas_call(
        pack_kernel,
        out_shape=jax.ShapeDtypeStruct((2, 8, 2, tokens, 512), slots.dtype),
        in_specs=[smem, smem, vmem],
        out_specs=vmem,
        scratch_shapes=[pltpu.SMEM((32,), jnp.int32)],
        cost_estimate=pl.CostEstimate(flops=1_000_000, bytes_accessed=5_000_000, transcendentals=0),
        name="pack",
    )(place, lengths, slots)


def unpack_kernel(place_ref, lengths_ref, weights_ref, out_ref, windows_ref):
    group = pl.program_id(0)
    replica = 8 * (group // 2) + 2 * place_ref[1] + group % 2
    pieces, blocks, rows, width = weights_ref.shape
    lane = lax.broadcasted_iota(jnp.int32, (pieces, rows, width), 2)

    @pl.when(group == 0)
    def _():
        def turned(t):
            tile = weights_ref[:, t].reshape(pieces * rows, width)
            return pltpu.roll(tile.astype(jnp.float32), UNIT, 1).reshape(pieces, rows, width)

        def window(t, low):
            high = turned(jnp.minimum(t + 1, blocks - 1))
            windows_ref[2 * t] = weights_ref[:, t]
            windows_ref[2 * t + 1] = jnp.where(lane < UNIT, low, high).astype(windows_ref.dtype)
            return high

        lax.fori_loop(0, blocks, window, turned(0), unroll=True)

    def slot(j, begin):
        count = lengths_ref[replica, j] // UNIT
        for k in range(2):
            value = windows_ref[jnp.minimum(begin + 2 * k, 2 * blocks - 1)]
            keep = lane < (count - 2 * k) * UNIT
            out_ref[j, :, :, width * k : width * (k + 1)] = jnp.where(keep, value, jnp.zeros_like(value))
        return begin + count

    lax.fori_loop(0, 16, slot, jnp.int32(0), unroll=True)


def slot_columns(weights, lengths, place):
    pieces, blocks, rows, width = weights.shape
    smem = pl.BlockSpec(memory_space=pltpu.SMEM)
    return pl.pallas_call(
        unpack_kernel,
        out_shape=jax.ShapeDtypeStruct((64, pieces, rows, 256), weights.dtype),
        grid=(4,),
        in_specs=[smem, smem, pl.BlockSpec((pieces, blocks, rows, width), lambda g: (0, 0, 0, 0))],
        out_specs=pl.BlockSpec((16, pieces, rows, 256), lambda g: (g, 0, 0, 0)),
        scratch_shapes=[pltpu.VMEM((2 * blocks, pieces, rows, width), weights.dtype)],
        cost_estimate=pl.CostEstimate(flops=3_000_000 * pieces, bytes_accessed=1_300_000 * pieces, transcendentals=0),
        name="unpack",
    )(place, lengths, weights)


def ring(step):
    return [(k, (k + step) % 8) for k in range(8)]


def all_rows(weights, ahead):
    yl, z = lax.axis_index("yl"), lax.axis_index(Z)
    other = lax.ppermute(weights, "yl", SWAP)
    pair = jnp.stack([jnp.where(yl == 0, weights, other), jnp.where(yl == 0, other, weights)])
    out = jnp.zeros((2, 8, *weights.shape), weights.dtype)

    def put(out, piece, first, distance):
        return lax.dynamic_update_slice(out, piece[:, None], (first, (z + distance) % 8, 0, 0))

    out = put(out, pair, 0, 0)
    up, down = pair, pair
    for k in range(1, 4):
        up = lax.ppermute(up, Z, ring(1))
        down = lax.ppermute(down, Z, ring(-1))
        out = put(out, up, 0, 8 - k)
        out = put(out, down, 0, k)
    up, down, ahead = lax.optimization_barrier((up, down, ahead))
    up = lax.ppermute(up[:1], Z, ring(1))
    down = lax.ppermute(down[1:], Z, ring(-1))
    out = put(out, up, 0, 4)
    out = put(out, down, 1, 4)
    return out.reshape(-1, weights.shape[1]), ahead


def product(tokens, dense):
    return lax.dot_general(tokens, dense, (((0,), (0,)), ((), ())), preferred_element_type=jnp.float32)


def on_device(tokens, grad_out, lengths, master, first, second):
    z0 = lax.axis_index("z0")
    place = jnp.stack([lax.axis_index(REP), lax.axis_index("zh")]).astype(jnp.int32)
    token_count, slot_width = grad_out.shape

    across = lax.ppermute(tokens, "z0", SWAP)
    own = [tokens, across]
    theirs = [lax.ppermute(part, "co", SWAP) for part in own]

    parts = grad_out.reshape(16, token_count // 16, slot_width)
    slots = lax.all_to_all(parts, TP, split_axis=0, concat_axis=0, tiled=True)
    spread = packed_columns(slots, lengths, place).reshape(32, token_count // 16, 512)
    dense = lax.all_to_all(spread, PAIR, split_axis=0, concat_axis=0, tiled=True)
    dense = dense.reshape(2, token_count, 512)
    columns = [lax.dynamic_index_in_dim(dense, z0 ^ k, 0, False) for k in range(2)]
    totals = [
        sum(product(t, d) for t, d in zip(features, columns)).astype(jnp.bfloat16)
        for features in (own, theirs)
    ]
    blocks = []
    for yl in range(2):
        for zh in range(4):
            half, part = sum_block(yl, zh)
            blocks.append(totals[half][:, 128 * part : 128 * (part + 1)])
    arrived = lax.all_to_all(jnp.stack(blocks), SUM, split_axis=0, concat_axis=0, tiled=True)
    summed = jnp.sum(arrived.astype(jnp.float32), axis=0).astype(jnp.bfloat16)
    gradient = lax.ppermute(summed, AXES, home_permutation())
    gradient = with_layout_constraint(gradient, Layout(major_to_minor=(0, 1))).astype(jnp.float32)

    new_master, new_first, new_second = adam_update(master, first, second, gradient)
    weights = new_master.astype(jnp.bfloat16)

    rows = lax.all_to_all(weights.reshape(16, 32, 128), TP, split_axis=0, concat_axis=0, tiled=True)
    others = []
    for step in (3, 2, 1):
        others.append(lax.ppermute(rows, "zh", [(k, (k + step) % 4) for k in range(4)]))
    zh = lax.axis_index("zh")
    slot_weights = jnp.zeros((2, 4, 2, 16, 32, slot_width), weights.dtype)
    healthy = None
    distance = 0
    for pieces in (rows[None], jnp.stack(others)):
        outgoing = slot_columns(pieces, lengths, place)
        incoming = lax.all_to_all(outgoing, GROUP, split_axis=0, concat_axis=0, tiled=True)
        incoming = incoming.reshape(2, 2, 16, -1, 32, slot_width).transpose(0, 3, 1, 2, 4, 5)
        for piece in range(incoming.shape[1]):
            slot_weights = lax.dynamic_update_slice(
                slot_weights, incoming[:, piece : piece + 1], (0, (zh + distance) % 4, 0, 0, 0, 0)
            )
            distance += 1
        if healthy is None:
            healthy, slot_weights = all_rows(weights, slot_weights)
    slot_weights = slot_weights.reshape(1, -1, slot_width)
    return (new_master, new_first, new_second, healthy, slot_weights)


def solution(mesh):
    torus = Mesh(mesh.devices.reshape(2, 4, 2, 4, 2, 2), AXES)
    placed = (P(REP, TP), P(REP, TP), P(), P(REP, TP), P(REP, TP), P(REP, TP))

    return jax.shard_map(
        on_device,
        mesh=torus,
        in_specs=placed,
        out_specs=(P(REP, TP), P(REP, TP), P(REP, TP), P(None, TP), P(REP, None, TP)),
        check_vma=False,
    )
```

```python
import jax
import jax.numpy as jnp
from jax import lax
from jax.experimental import pallas as pl
from jax.experimental.pallas import tpu as pltpu
from jax.experimental.layout import Layout, with_layout_constraint
from jax.sharding import Mesh
from jax.sharding import PartitionSpec as P

STEP = 1000
UNIT = 64
AXES = ("yl", "zh", "z0", "x", "yh", "co")
REP = ("yl", "zh", "z0")
TP = ("x", "yh", "co")
Z = ("zh", "z0")
PAIR = ("z0", "x", "yh", "co")
GROUP = ("yl", "z0", "x", "yh", "co")
SUM = ("yl", "zh")
SWAP = [(0, 1), (1, 0)]

decay_first = 0.9
decay_second = 0.999
learning_rate = 0.02
weight_decay = 0.1
epsilon = 1e-08


def adam_update(master, first, second, gradient):
    scale_first = 1.0 - decay_first**STEP
    scale_second = 1.0 - decay_second**STEP
    new_first = decay_first * first + (1.0 - decay_first) * gradient
    new_second = decay_second * second + (1.0 - decay_second) * gradient * gradient
    direction = new_first / scale_first / (jnp.sqrt(new_second / scale_second) + epsilon)
    new_master = master - learning_rate * (direction + weight_decay * master)
    return (new_master, new_first, new_second)


def sum_block(yl, zh):
    return zh // 2, 2 * yl + zh % 2


def column_block(z0, co, x, yh):
    return 2 * (z0 ^ (x % 2)) + (co ^ (x % 2) ^ yh)


def home_permutation():
    pairs = []
    for yl in range(2):
        for zh in range(4):
            for z0 in range(2):
                for x in range(4):
                    for yh in range(2):
                        for co in range(2):
                            half, part = sum_block(yl, zh)
                            source = ((((yl * 4 + zh) * 2 + z0) * 4 + x) * 2 + yh) * 2 + co
                            row = 4 * x + 2 * yh + (co ^ half)
                            col = 4 * column_block(z0, co, x, yh) + part
                            pairs.append((source, row * 16 + col))
    return pairs


def swapped_halves(tile):
    return pltpu.roll(tile.astype(jnp.float32), UNIT, 1)


def pack_kernel(place_ref, lengths_ref, slots_ref, out_ref, table_ref):
    replica = place_ref[0]
    begin = jnp.int32(0)
    for j in range(16):
        count = lengths_ref[replica, j] // UNIT
        for k in range(4):

            @pl.when(k < count)
            def _(begin=begin, j=j, k=k):
                table_ref[begin + k] = jnp.int32(4 * j + k)

        begin = begin + count
    lane = lax.broadcasted_iota(jnp.int32, (slots_ref.shape[1], 128), 1)

    def tile_of(unit):
        return slots_ref[unit // 4, :, pl.ds(pl.multiple_of((unit // 2) % 2 * 128, 128), 128)]

    for d in range(16):
        left, right = table_ref[2 * d], table_ref[2 * d + 1]
        tile_l, tile_r = tile_of(left), tile_of(right)
        low = jnp.where(left % 2 == 0, tile_l.astype(jnp.float32), swapped_halves(tile_l))
        high = jnp.where(right % 2 == 1, tile_r.astype(jnp.float32), swapped_halves(tile_r))
        dense = jnp.where(lane < UNIT, low, high).astype(out_ref.dtype)
        block, part = d // 4, 128 * (d % 4)
        for x in range(4):
            for yh in range(2):
                for z0 in range(2):
                    for co in range(2):
                        if column_block(z0, co, x, yh) == block:
                            out_ref[z0, 2 * x + yh, co, :, part : part + 128] = dense


def packed_columns(slots, lengths, place):
    tokens = slots.shape[1]
    smem = pl.BlockSpec(memory_space=pltpu.SMEM)
    vmem = pl.BlockSpec(memory_space=pltpu.VMEM)
    return pl.pallas_call(
        pack_kernel,
        out_shape=jax.ShapeDtypeStruct((2, 8, 2, tokens, 512), slots.dtype),
        in_specs=[smem, smem, vmem],
        out_specs=vmem,
        scratch_shapes=[pltpu.SMEM((32,), jnp.int32)],
        cost_estimate=pl.CostEstimate(flops=1_000_000, bytes_accessed=5_000_000, transcendentals=0),
        name="pack",
    )(place, lengths, slots)


def unpack_kernel(place_ref, lengths_ref, weights_ref, out_ref, windows_ref):
    group = pl.program_id(0)
    replica = 8 * (group // 2) + 2 * place_ref[1] + group % 2
    pieces, blocks, rows, width = weights_ref.shape
    lane = lax.broadcasted_iota(jnp.int32, (pieces, rows, width), 2)

    @pl.when(group == 0)
    def _():
        def turned(t):
            tile = weights_ref[:, t].reshape(pieces * rows, width)
            return pltpu.roll(tile.astype(jnp.float32), UNIT, 1).reshape(pieces, rows, width)

        def window(t, low):
            high = turned(jnp.minimum(t + 1, blocks - 1))
            windows_ref[2 * t] = weights_ref[:, t]
            windows_ref[2 * t + 1] = jnp.where(lane < UNIT, low, high).astype(windows_ref.dtype)
            return high

        lax.fori_loop(0, blocks, window, turned(0), unroll=True)

    def slot(j, begin):
        count = lengths_ref[replica, j] // UNIT
        for k in range(2):
            value = windows_ref[jnp.minimum(begin + 2 * k, 2 * blocks - 1)]
            keep = lane < (count - 2 * k) * UNIT
            out_ref[j, :, :, width * k : width * (k + 1)] = jnp.where(keep, value, jnp.zeros_like(value))
        return begin + count

    lax.fori_loop(0, 16, slot, jnp.int32(0), unroll=True)


def slot_columns(weights, lengths, place):
    pieces, blocks, rows, width = weights.shape
    smem = pl.BlockSpec(memory_space=pltpu.SMEM)
    return pl.pallas_call(
        unpack_kernel,
        out_shape=jax.ShapeDtypeStruct((64, pieces, rows, 256), weights.dtype),
        grid=(4,),
        in_specs=[smem, smem, pl.BlockSpec((pieces, blocks, rows, width), lambda g: (0, 0, 0, 0))],
        out_specs=pl.BlockSpec((16, pieces, rows, 256), lambda g: (g, 0, 0, 0)),
        scratch_shapes=[pltpu.VMEM((2 * blocks, pieces, rows, width), weights.dtype)],
        cost_estimate=pl.CostEstimate(flops=3_000_000 * pieces, bytes_accessed=1_300_000 * pieces, transcendentals=0),
        name="unpack",
    )(place, lengths, weights)


def ring(step):
    return [(k, (k + step) % 8) for k in range(8)]


def all_rows(weights):
    yl, z = lax.axis_index("yl"), lax.axis_index(Z)
    other = lax.ppermute(weights, "yl", SWAP)
    pair = jnp.stack([jnp.where(yl == 0, weights, other), jnp.where(yl == 0, other, weights)])
    out = jnp.zeros((2, 8, *weights.shape), weights.dtype)

    def put(out, piece, first, distance):
        return lax.dynamic_update_slice(out, piece[:, None], (first, (z + distance) % 8, 0, 0))

    out = put(out, pair, 0, 0)
    up, down = pair, pair
    for k in range(1, 4):
        up = lax.ppermute(up, Z, ring(1))
        down = lax.ppermute(down, Z, ring(-1))
        out = put(out, up, 0, 8 - k)
        out = put(out, down, 0, k)
    up = lax.ppermute(up[:1], Z, ring(1))
    down = lax.ppermute(down[1:], Z, ring(-1))
    out = put(out, up, 0, 4)
    out = put(out, down, 1, 4)
    return out.reshape(-1, weights.shape[1])


def product(tokens, dense):
    return lax.dot_general(tokens, dense, (((0,), (0,)), ((), ())), preferred_element_type=jnp.float32)


def on_device(tokens, grad_out, lengths, master, first, second):
    z0 = lax.axis_index("z0")
    place = jnp.stack([lax.axis_index(REP), lax.axis_index("zh")]).astype(jnp.int32)
    token_count, slot_width = grad_out.shape

    across = lax.ppermute(tokens, "z0", SWAP)
    own = [tokens, across]
    theirs = [lax.ppermute(part, "co", SWAP) for part in own]

    parts = grad_out.reshape(16, token_count // 16, slot_width)
    slots = lax.all_to_all(parts, TP, split_axis=0, concat_axis=0, tiled=True)
    spread = packed_columns(slots, lengths, place).reshape(32, token_count // 16, 512)
    dense = lax.all_to_all(spread, PAIR, split_axis=0, concat_axis=0, tiled=True)
    dense = dense.reshape(2, token_count, 512)
    columns = [lax.dynamic_index_in_dim(dense, z0 ^ k, 0, False) for k in range(2)]
    totals = [
        sum(product(t, d) for t, d in zip(features, columns)).astype(jnp.bfloat16)
        for features in (own, theirs)
    ]
    blocks = []
    for yl in range(2):
        for zh in range(4):
            half, part = sum_block(yl, zh)
            blocks.append(totals[half][:, 128 * part : 128 * (part + 1)])
    arrived = lax.all_to_all(jnp.stack(blocks), SUM, split_axis=0, concat_axis=0, tiled=True)
    summed = jnp.sum(arrived.astype(jnp.float32), axis=0).astype(jnp.bfloat16)
    gradient = lax.ppermute(summed, AXES, home_permutation())
    gradient = with_layout_constraint(gradient, Layout(major_to_minor=(0, 1))).astype(jnp.float32)

    new_master, new_first, new_second = adam_update(master, first, second, gradient)
    weights = new_master.astype(jnp.bfloat16)

    rows = lax.all_to_all(weights.reshape(16, 32, 128), TP, split_axis=0, concat_axis=0, tiled=True)
    others = [lax.ppermute(rows, "zh", [(k, (k + step) % 4) for k in range(4)]) for step in (3, 2, 1)]
    zh = lax.axis_index("zh")
    slot_weights = None
    distance = 0
    for pieces in (rows[None], jnp.stack(others)):
        outgoing = slot_columns(pieces, lengths, place)
        incoming = lax.all_to_all(outgoing, GROUP, split_axis=0, concat_axis=0, tiled=True)
        incoming = incoming.reshape(2, 2, 16, -1, 32, slot_width).transpose(0, 3, 1, 2, 4, 5)
        if slot_weights is None:
            slot_weights = jnp.broadcast_to(incoming, (2, 4, *incoming.shape[2:]))
            distance = 1
            continue
        for piece in range(incoming.shape[1]):
            slot_weights = lax.dynamic_update_slice(
                slot_weights, incoming[:, piece : piece + 1], (0, (zh + distance) % 4, 0, 0, 0, 0)
            )
            distance += 1
    slot_weights = slot_weights.reshape(1, -1, slot_width)
    healthy = all_rows(weights)
    return (new_master, new_first, new_second, healthy, slot_weights)


def solution(mesh):
    torus = Mesh(mesh.devices.reshape(2, 4, 2, 4, 2, 2), AXES)
    placed = (P(REP, TP), P(REP, TP), P(), P(REP, TP), P(REP, TP), P(REP, TP))

    return jax.shard_map(
        on_device,
        mesh=torus,
        in_specs=placed,
        out_specs=(P(REP, TP), P(REP, TP), P(REP, TP), P(None, TP), P(REP, None, TP)),
        check_vma=False,
    )
```
